1024 devices in a mesh: gx: 8 (over x), gy: 8 (over z), gz: 16 (over y, core).
Axes of the slice: x: 8, y: 8, z: 8, core: 2. Of those that a mesh axis runs over, the one named last changes fastest.
Arguments:
- offsets: float32 [3, 16, 16, 32, 128], P(None, 'gx', 'gy', 'gz'), may hold values from 0 to 1
- masses: float32 [16, 16, 32, 128], P('gx', 'gy', 'gz'), may hold values from 0.12 to 3
- smoothing: float32 [16, 16, 32, 128], P('gx', 'gy', 'gz'), may hold values from 0.6 to 0.75
- velocity: float32 [3, 16, 16, 32, 128], P(None, 'gx', 'gy', 'gz'), may hold values from -6 to 6
- energy: float32 [16, 16, 32, 128], P('gx', 'gy', 'gz'), may hold values from 0.3 to 3
- active: int32 [16, 16, 32, 128], P('gx', 'gy', 'gz'), may hold values from 0 to 1, as said below
Outputs:
- density: float32 [16, 16, 32, 128], P('gx', 'gy', 'gz')
- acceleration: float32 [3, 16, 16, 32, 128], P(None, 'gx', 'gy', 'gz')
- heating: float32 [16, 16, 32, 128], P('gx', 'gy', 'gz')
The draws below stay inside these ranges and needn't reach their ends.
Inputs may be any that keep to these rules, and one draw needn't show every extreme that they name: The share of active particles differs from cell to cell, from none to all.
All inputs are finite; a program needn't handle non-finite values.
Results may differ from the reference program's by a relative error of at most 0.0003.
Values sent between devices are 32-bit elements; how exact they have to be, the bound alone decides.
A program may use at most 32 MiB of HBM per device.

```python
import math
import jax
import jax.numpy as jnp
from jax import lax

P_SIZE = 128
PASSES = 2
NCX = 16
NCY = 16
NCZ = 32


def draw_active(key, part):
    levels = jax.random.randint(jax.random.fold_in(key, 11), (NCX, NCY, NCZ, 1), 0, 9)
    tickets = jax.random.randint(jax.random.fold_in(key, 12), (NCX, NCY, NCZ, P_SIZE), 0, 8)
    return (tickets < levels).astype(jnp.int32)


def draw_masses(key, part):
    shape = (NCX, NCY, NCZ, P_SIZE)
    tickets = jax.random.randint(jax.random.fold_in(key, 21), shape, 0, 16)
    heavy = tickets == 0
    light_mass = jnp.exp(jax.random.uniform(jax.random.fold_in(key, 22), shape, jnp.float32, math.log(0.12), math.log(0.2)))
    heavy_mass = jnp.exp(jax.random.uniform(jax.random.fold_in(key, 23), shape, jnp.float32, math.log(2.4), math.log(3.0)))
    chosen = jnp.where(heavy, heavy_mass, light_mass)
    return jnp.clip(chosen, 0.12, 3.0).astype(jnp.float32)


def steps_of(stream_key, extent, cuts, least, top_value):
    def one(axis_at, shards_of):
        draws = jax.random.uniform(jax.random.fold_in(jax.random.fold_in(stream_key, 6), axis_at), (shards_of,), jnp.float32, least / len(cuts), top_value / len(cuts))
        return jnp.repeat(jnp.exp(draws), extent[axis_at] // shards_of).reshape((-1,) + (1,) * (len(extent) - axis_at - 1))

    level = one(*cuts[0])
    for cut in cuts[1:]:
        level = level * one(*cut)
    return level


def noise(own_key, extent, width, bound, split=(), held_as=jnp.bfloat16):
    drawn = jax.random.normal(own_key, extent, jnp.float32) * width
    if len(split) > 0:
        drawn = steps_of(own_key, extent, split, -0.22, 0.18) * drawn
    return jnp.clip(drawn, min=-bound, max=bound).astype(held_as)


def setup_inputs(seed: int = 0) -> dict:
    splits = jax.random.split(jax.random.key(seed), 7)
    return {
        "offsets": jnp.clip(1.0 * jax.random.uniform(splits[0], (3, NCX, NCY, NCZ, P_SIZE), jnp.float32) ** steps_of(splits[0], (3, NCX, NCY, NCZ, P_SIZE), ((1, 8), (2, 8), (3, 16)), -0.2, 0.2), 0.0, 1.0),
        "masses": draw_masses(jax.random.fold_in(splits[6], 71), 0),
        "smoothing": jnp.clip(0.6 + 0.14999998 * jax.random.uniform(splits[2], (NCX, NCY, NCZ, P_SIZE), jnp.float32) ** steps_of(splits[2], (NCX, NCY, NCZ, P_SIZE), ((0, 8), (1, 8), (2, 16)), -0.2, 0.2), 0.6, 0.75),
        "velocity": noise(splits[3], (3, NCX, NCY, NCZ, P_SIZE), 1.0, 6.0, ((1, 8), (2, 8), (3, 16)), jnp.float32),
        "energy": jnp.clip(jnp.exp(math.log(3.0) - 2.3025851 * jax.random.uniform(splits[4], (NCX, NCY, NCZ, P_SIZE), jnp.float32) ** steps_of(splits[4], (NCX, NCY, NCZ, P_SIZE), ((0, 8), (1, 8), (2, 16)), -0.2, 0.2)), 0.3, 3.0),
        "active": draw_active(jax.random.fold_in(splits[6], 71), 0),
    }


kernel_norm = 2.5464790894703255
eta_factor = 2.3
gamma_index = 5.0 / 3.0

def kernel(radius, length):
    scaled = radius / length
    remain = 1.0 - scaled
    inner_part = 1.0 - 6.0 * scaled * scaled + 6.0 * scaled * scaled * scaled
    outer_part = 2.0 * remain * remain * remain
    profile = jnp.where(scaled < 0.5, inner_part, jnp.where(scaled < 1.0, outer_part, 0.0))
    return kernel_norm * profile / (length * length * length)

def slope(radius, length):
    scaled = radius / length
    remain = 1.0 - scaled
    inner_part = 18.0 * scaled - 12.0
    outer_part = -6.0 * remain * remain / jnp.maximum(scaled, 0.5)
    profile = jnp.where(scaled < 0.5, inner_part, jnp.where(scaled < 1.0, outer_part, 0.0))
    square = length * length
    return kernel_norm * profile / (square * square * length)

def window(member, shift_x, shift_y, shift_z, count_y, count_z):
    return member[..., shift_x:shift_x + 1, shift_y:shift_y + count_y, shift_z:shift_z + count_z, :]

def separation(target_off, source_off, shift_x, shift_y, shift_z):
    count_y = target_off.shape[2]
    count_z = target_off.shape[3]
    source_slab = window(source_off, shift_x, shift_y, shift_z, count_y, count_z)
    deltas = []
    for component, offset_cell in enumerate((shift_x, shift_y, shift_z)):
        deltas.append(target_off[component][..., :, None] - source_slab[component][..., None, :] - (offset_cell - 1.0))
    radius = jnp.sqrt(deltas[0] * deltas[0] + deltas[1] * deltas[1] + deltas[2] * deltas[2])
    return (deltas, radius)

def density_slab(targets, sources):
    target_off, length = targets
    source_off, source_mass = sources
    count_y = length.shape[1]
    count_z = length.shape[2]
    summed = jnp.zeros(length.shape, jnp.float32)
    for shift_x in range(3):
        for shift_y in range(3):
            for shift_z in range(3):
                deltas, radius = separation(target_off, source_off, shift_x, shift_y, shift_z)
                weight = window(source_mass, shift_x, shift_y, shift_z, count_y, count_z)
                summed = summed + lax.optimization_barrier(jnp.sum(weight[..., None, :] * kernel(radius, length[..., None]), axis=-1))
    return (summed,)

def force_slab(targets, sources):
    target_off, length, density_now, veloc, energy_now = targets
    source_off, source_mass, source_len, source_dens, source_vel, source_energy = sources
    count_y = length.shape[1]
    count_z = length.shape[2]
    pressure = (gamma_index - 1.0) * energy_now / density_now
    source_press = (gamma_index - 1.0) * source_energy / source_dens
    pushes = [jnp.zeros(length.shape, jnp.float32) for component in range(3)]
    heating = jnp.zeros(length.shape, jnp.float32)
    for shift_x in range(3):
        for shift_y in range(3):
            for shift_z in range(3):
                deltas, radius = separation(target_off, source_off, shift_x, shift_y, shift_z)
                mass_j = window(source_mass, shift_x, shift_y, shift_z, count_y, count_z)[..., None, :]
                press_j = window(source_press, shift_x, shift_y, shift_z, count_y, count_z)[..., None, :]
                len_j = window(source_len, shift_x, shift_y, shift_z, count_y, count_z)[..., None, :]
                vel_j = window(source_vel, shift_x, shift_y, shift_z, count_y, count_z)
                own_slope = slope(radius, length[..., None])
                their_slope = slope(radius, len_j)
                coupling = mass_j * (pressure[..., None] * own_slope + press_j * their_slope)
                approach = deltas[0] * (veloc[0][..., :, None] - vel_j[0][..., None, :])
                approach = approach + deltas[1] * (veloc[1][..., :, None] - vel_j[1][..., None, :])
                approach = approach + deltas[2] * (veloc[2][..., :, None] - vel_j[2][..., None, :])
                heating = heating + lax.optimization_barrier(jnp.sum(mass_j * own_slope * approach, axis=-1))
                for component in range(3):
                    pushes[component] = pushes[component] - lax.optimization_barrier(jnp.sum(coupling * deltas[component], axis=-1))
    return (jnp.stack(pushes), pressure * heating)

def sweep(kernel_fn, targets, sources):
    count = targets[1].shape[0]

    def one_slab(first_slab):
        parts_t = tuple((lax.dynamic_slice_in_dim(member, first_slab, 1, member.ndim - 4) for member in targets))
        parts_s = tuple((lax.dynamic_slice_in_dim(member, first_slab, 3, member.ndim - 4) for member in sources))
        return kernel_fn(parts_t, parts_s)
    stacked = lax.map(one_slab, jnp.arange(count, dtype=jnp.int32))
    results = []
    for member in stacked:
        flat = jnp.squeeze(member, axis=member.ndim - 4)
        results.append(jnp.moveaxis(flat, 0, flat.ndim - 4))
    return tuple(results)

def settle(target_off, target_mass, length, source_off, source_mass):
    density_now = length
    for pass_index in range(PASSES):
        density_now, = sweep(density_slab, (target_off, length), (source_off, source_mass))
        length = eta_factor * jnp.cbrt(target_mass / density_now)
    return (length, density_now)

def wrap(field):
    widths = [(0, 0)] * (field.ndim - 4) + [(1, 1), (1, 1), (1, 1), (0, 0)]
    return jnp.pad(field, widths, mode='wrap')

def reference(offsets, masses, smoothing, velocity, energy, active):
    pad_off = wrap(offsets)
    pad_mass = wrap(masses)
    length, density_now = settle(offsets, masses, smoothing, pad_off, pad_mass)
    sources = (pad_off, pad_mass, wrap(length), wrap(density_now), wrap(velocity), wrap(energy))
    pushes, heating = sweep(force_slab, (offsets, length, density_now, velocity, energy), sources)
    active_weight = active.astype(jnp.float32)
    return (density_now, pushes * active_weight, heating * active_weight)
```

```python
import functools

import jax
import jax.numpy as jnp
from jax import lax
from jax.experimental import pallas as pl
from jax.experimental.pallas import tpu as pltpu
from jax.sharding import PartitionSpec as P

MESH = pl.DeviceIdType.MESH
AXES = ("gx", "gy", "gz")
KERNEL_NORM = 2.5464790894703255
ETA = 2.3
GAMMA = 5.0 / 3.0
ROOT3 = 3.0**0.5
TINY = 1e-12
DIRECTIONS = [
    (dx, dy, dz) for dx in (-1, 0, 1) for dy in (-1, 0, 1) for dz in (-1, 0, 1) if (dx, dy, dz) != (0, 0, 0)
]
OFFSETS = [(a * 16 + b * 4 + c) for a in range(3) for b in range(3) for c in range(3)]


def source_part(step):
    return slice(2, 3) if step == 1 else slice(1, 2) if step == -1 else slice(1, 3)


def landing_part(step):
    return slice(0, 1) if step == 1 else slice(3, 4) if step == -1 else slice(1, 3)


def neighbour(direction):
    found = {}
    for axis, step in zip(AXES, direction):
        count = lax.axis_size(axis)
        found[axis] = lax.rem(lax.axis_index(axis) + count + step, count)
    return tuple(found[axis] for axis in AXES)


def exchange(buffer, send_sem, recv_sem):
    copies = []
    for place, direction in enumerate(DIRECTIONS):
        here = tuple(source_part(step) for step in direction)
        there = tuple(landing_part(step) for step in direction)
        copies.append(
            pltpu.make_async_remote_copy(
                src_ref=buffer.at[here],
                dst_ref=buffer.at[there],
                send_sem=send_sem.at[place],
                recv_sem=recv_sem.at[place],
                device_id=neighbour(direction),
                device_id_type=MESH,
            )
        )
    return copies


def rounded(value):
    return value.astype(jnp.bfloat16).astype(jnp.float32)


def thirds(value):
    high = rounded(value)
    rest = value - high
    middle = rounded(rest)
    return high, middle, rest - middle


def cube_root(value):
    guess = jnp.exp(jnp.log(value) * (1.0 / 3.0))
    return (2.0 * guess + value / (guess * guess)) * (1.0 / 3.0)


def fold(tile):
    parts = [tile[8 * i : 8 * i + 8] for i in range(tile.shape[0] // 8)]
    while len(parts) > 1:
        parts = [parts[i] + parts[i + 1] for i in range(0, len(parts) - 1, 2)] + (
            [parts[-1]] if len(parts) % 2 else []
        )
    return parts[0]


def placed(tile, cell_x, cell_y, cell_z):
    row = lax.broadcasted_iota(jnp.int32, (8, 128), 0)
    shift = jnp.where(
        row == 0,
        cell_x.astype(jnp.float32) - 2.0,
        jnp.where(row == 1, cell_y.astype(jnp.float32) - 2.0, jnp.where(row == 2, cell_z.astype(jnp.float32) - 2.0, 0.0)),
    )
    return row, tile + shift


def kernel(
    off_ref,
    mass_ref,
    smooth_ref,
    vel_ref,
    energy_ref,
    active_ref,
    dens_ref,
    acc_ref,
    heat_ref,
    field,
    late,
    feat,
    tfeat,
    mass_b,
    len_b,
    col_a,
    col_b,
    dist,
    square,
    send_sem,
    recv_sem,
    send_late,
    recv_late,
):
    f32 = jnp.float32
    barrier = pltpu.get_barrier_semaphore()
    for direction in DIRECTIONS:
        pl.semaphore_signal(barrier, inc=1, device_id=neighbour(direction), device_id_type=MESH)
    for x in range(2):
        for y in range(2):
            for z in range(2):
                for c in range(3):
                    field[1 + x, 1 + y, 1 + z, c : c + 1] = off_ref[c, x, y, z : z + 1]
                    field[1 + x, 1 + y, 1 + z, 4 + c : 5 + c] = vel_ref[c, x, y, z : z + 1]
                field[1 + x, 1 + y, 1 + z, 3:4] = mass_ref[x, y, z : z + 1]
                field[1 + x, 1 + y, 1 + z, 7:8] = energy_ref[x, y, z : z + 1]
    pl.semaphore_wait(barrier, len(DIRECTIONS))
    first = exchange(field, send_sem, recv_sem)
    for copy in first:
        copy.start()

    lane_row = lax.broadcasted_iota(jnp.int32, (48, 128), 0)
    pick = jnp.where((lane_row == 5) | (lane_row == 29) | (lane_row == 45), 1.0, 0.0).astype(jnp.bfloat16)

    for copy in first:
        copy.wait()

    def prepare(cell, carry):
        cell_x, cell_y, cell_z = cell // 16, (cell // 4) % 4, cell % 4
        tile = field[cell_x, cell_y, cell_z]
        row, where_at = placed(tile, cell_x, cell_y, cell_z)
        mass = tile[3:4]
        norm = jnp.sum(jnp.where(row < 3, where_at * where_at, 0.0), axis=0, keepdims=True)
        moving = jnp.sum(jnp.where(row < 3, where_at * pltpu.roll(tile, 4, 0), 0.0), axis=0, keepdims=True)
        given = jnp.where(
            row < 3,
            where_at,
            jnp.where(row == 3, norm, jnp.where(row == 4, 1.0, jnp.where(row == 5, mass, 0.0))),
        )
        high, middle, low = thirds(given)
        stack = jnp.concatenate([high, high, high, middle, middle, low], axis=0)
        turned = jnp.transpose(stack).astype(jnp.bfloat16)
        feat[cell] = turned
        mass_b[cell] = jnp.dot(turned, pick, preferred_element_type=f32)
        column = jnp.where(row == 3, 1.0, jnp.where(row == 7, moving, where_at)) * mass
        high, middle, low = thirds(column)
        upper = jnp.concatenate([high, middle, low, jnp.zeros_like(low)], axis=0).astype(jnp.bfloat16)
        lower = jnp.concatenate([high, middle, jnp.zeros_like(low), jnp.zeros_like(low)], axis=0).astype(jnp.bfloat16)
        col_a[cell] = jnp.concatenate([upper, lower], axis=1)
        return carry

    lax.fori_loop(0, 64, prepare, 0)

    def density_of(total, length):
        cube = length * length * length
        return (2.0 * KERNEL_NORM) * jnp.sum(total, axis=0, keepdims=True) / (cube * cube)

    def parts_of(target):
        return target // 4, (target // 2) % 2, target % 2

    def base_of(target):
        tx, ty, tz = parts_of(target)
        return tx * 16 + ty * 4 + tz

    def weigh(radius, three_square, length, half, half_cube):
        gap = jnp.maximum(length - radius, 0.0)
        return jnp.where(radius < half, half_cube - three_square * gap, gap * gap * gap)

    def target_fields(target):
        tx, ty, tz = parts_of(target)
        tile = field[1 + tx, 1 + ty, 1 + tz]
        row, where_at = placed(tile, 1 + tx, 1 + ty, 1 + tz)
        return tile, row, where_at

    def first_pass(target, carry):
        tx, ty, tz = parts_of(target)
        tile, row, where_at = target_fields(target)
        norm = jnp.sum(jnp.where(row < 3, where_at * where_at, 0.0), axis=0, keepdims=True)
        given = jnp.where(row < 3, -2.0 * where_at, jnp.where(row == 3, 1.0, jnp.where(row == 4, norm, 0.0)))
        high, middle, low = thirds(given)
        target_feat = jnp.concatenate([high, middle, low, high, middle, high], axis=0).astype(jnp.bfloat16)
        length = smooth_ref[tx, ty, pl.ds(tz, 1)]
        half = 0.5 * length
        half_cube = half * length * length
        base = base_of(target)
        total = jnp.zeros((8, 128), f32)
        for place, offset in enumerate(OFFSETS):
            flat = jnp.maximum(jnp.dot(feat[base + offset], target_feat, preferred_element_type=f32), TINY)
            radius = flat * lax.rsqrt(flat)
            three_square = 3.0 * flat
            dist[target, place] = radius
            square[target, place] = three_square
            total = total + fold(mass_b[base + offset] * weigh(radius, three_square, length, half, half_cube))
        density = density_of(total, length)
        tfeat[target, 0:1] = ETA * cube_root(tile[3:4] / density)
        return carry

    lax.fori_loop(0, 8, first_pass, 0)

    def second_pass(target, carry):
        tx, ty, tz = parts_of(target)
        tile = field[1 + tx, 1 + ty, 1 + tz]
        mass, energy = tile[3:4], tile[7:8]
        length = tfeat[target, 0:1]
        half = 0.5 * length
        half_cube = half * length * length
        base = base_of(target)
        total = jnp.zeros((8, 128), f32)
        for place, offset in enumerate(OFFSETS):
            total = total + fold(
                mass_b[base + offset] * weigh(dist[target, place], square[target, place], length, half, half_cube)
            )
        density = density_of(total, length)
        length = ETA * cube_root(mass / density)
        dens_ref[tx, ty, pl.ds(tz, 1)] = density
        cube = length * length * length
        ratio = (GAMMA - 1.0) * energy / density / (cube * cube)
        tfeat[target, 1:2] = ratio
        late[1 + tx, 1 + ty, 1 + tz, 0:1] = length
        late[1 + tx, 1 + ty, 1 + tz, 1:2] = mass * ratio
        return carry

    lax.fori_loop(0, 8, second_pass, 0)

    second = exchange(late, send_late, recv_late)
    for copy in second:
        copy.start()
    for copy in second:
        copy.wait()

    def prepare_late(cell, carry):
        cell_x, cell_y, cell_z = cell // 16, (cell // 4) % 4, cell % 4
        row, where_at = placed(field[cell_x, cell_y, cell_z], cell_x, cell_y, cell_z)
        values = late[cell_x, cell_y, cell_z]
        len_b[cell] = jnp.transpose(jnp.broadcast_to(values[0:1], (128, 128)))
        column = jnp.where(row == 3, 1.0, jnp.where(row < 3, where_at, 0.0)) * values[1:2]
        high, middle, low = thirds(column)
        upper = jnp.concatenate([high, middle, low, jnp.zeros_like(low)], axis=0).astype(jnp.bfloat16)
        lower = jnp.concatenate([high, middle, jnp.zeros_like(low), jnp.zeros_like(low)], axis=0).astype(jnp.bfloat16)
        col_b[cell] = jnp.concatenate([upper, lower], axis=1)
        return carry

    lax.fori_loop(0, 64, prepare_late, 0)

    def halves(value):
        high = value.astype(jnp.bfloat16)
        low = (value - high.astype(f32)).astype(jnp.bfloat16)
        return jnp.concatenate([high, low], axis=0)

    def force(target, carry):
        tx, ty, tz = parts_of(target)
        tile, row, where_at = target_fields(target)
        length = late[1 + tx, 1 + ty, 1 + tz, 0:1]
        steep = (2.0 / ROOT3) * length
        base = base_of(target)
        own = jnp.zeros((32, 128), f32)
        theirs = jnp.zeros((32, 128), f32)
        for place, offset in enumerate(OFFSETS):
            radius = dist[target, place]
            inverse = lax.rsqrt(square[target, place])
            twice = radius + radius
            scaled = ROOT3 * radius
            gap = jnp.maximum(length - radius, 0.0)
            slope = jnp.where(twice < length, steep - scaled, gap * gap * inverse)
            own = own + jnp.dot(col_a[base + offset], halves(slope), preferred_element_type=f32)
            their_length = len_b[base + offset]
            gap = jnp.maximum(their_length - radius, 0.0)
            slope = jnp.where(
                twice < their_length, (2.0 / ROOT3) * their_length - scaled, gap * gap * inverse
            )
            theirs = theirs + jnp.dot(col_b[base + offset], halves(slope), preferred_element_type=f32)
        own = own[0:8] + (own[8:16] + own[16:24])
        theirs = theirs[0:8] + (theirs[8:16] + theirs[16:24])
        on = active_ref[tx, ty, pl.ds(tz, 1)].astype(f32)
        scale = (6.0 * ROOT3 * KERNEL_NORM) * on
        ratio = tfeat[target, 1:2]
        push = scale * (ratio * (where_at * own[3:4] - own) + (where_at * theirs[3:4] - theirs))
        for c in range(3):
            acc_ref[c, tx, ty, pl.ds(tz, 1)] = push[c : c + 1]
        speed = pltpu.roll(tile, 4, 0)
        slide = pltpu.roll(own, 4, 0)
        mixed = speed * (where_at * own[3:4] - own) - where_at * slide
        heat = jnp.sum(jnp.where(row < 3, mixed, 0.0), axis=0, keepdims=True) + own[7:8]
        heat_ref[tx, ty, pl.ds(tz, 1)] = -scale * ratio * heat
        return carry

    lax.fori_loop(0, 8, force, 0)


def body(offsets, masses, smoothing, velocity, energy, active):
    f32, bf16 = jnp.float32, jnp.bfloat16
    vmem = pl.BlockSpec(memory_space=pltpu.VMEM)
    count = len(DIRECTIONS)
    return pl.pallas_call(
        kernel,
        out_shape=(
            jax.ShapeDtypeStruct(masses.shape, f32),
            jax.ShapeDtypeStruct(offsets.shape, f32),
            jax.ShapeDtypeStruct(masses.shape, f32),
        ),
        in_specs=[vmem] * 6,
        out_specs=(vmem, vmem, vmem),
        scratch_shapes=[
            pltpu.VMEM((4, 4, 4, 8, 128), f32),
            pltpu.VMEM((4, 4, 4, 2, 128), f32),
            pltpu.VMEM((64, 128, 48), bf16),
            pltpu.VMEM((8, 8, 128), f32),
            pltpu.VMEM((64, 128, 128), f32),
            pltpu.VMEM((64, 128, 128), f32),
            pltpu.VMEM((64, 32, 256), bf16),
            pltpu.VMEM((64, 32, 256), bf16),
            pltpu.VMEM((8, 27, 128, 128), f32),
            pltpu.VMEM((8, 27, 128, 128), f32),
            pltpu.SemaphoreType.DMA((count,)),
            pltpu.SemaphoreType.DMA((count,)),
            pltpu.SemaphoreType.DMA((count,)),
            pltpu.SemaphoreType.DMA((count,)),
        ],
        compiler_params=pltpu.CompilerParams(collective_id=0, has_side_effects=True, vmem_limit_bytes=60 * 1024 * 1024),
    )(offsets, masses, smoothing, velocity, energy, active)


def solution(mesh):
    in_specs = (
        P(None, "gx", "gy", "gz", None),
        P("gx", "gy", "gz", None),
        P("gx", "gy", "gz", None),
        P(None, "gx", "gy", "gz", None),
        P("gx", "gy", "gz", None),
        P("gx", "gy", "gz", None),
    )
    out_specs = (
        P("gx", "gy", "gz", None),
        P(None, "gx", "gy", "gz", None),
        P("gx", "gy", "gz", None),
    )
    return jax.shard_map(body, mesh=mesh, in_specs=in_specs, out_specs=out_specs, check_vma=False)
```

```python
import functools

import jax
import jax.numpy as jnp
from jax import lax
from jax.experimental import pallas as pl
from jax.experimental.pallas import tpu as pltpu
from jax.sharding import PartitionSpec as P

MESH = pl.DeviceIdType.MESH
AXES = ("gx", "gy", "gz")
KERNEL_NORM = 2.5464790894703255
ETA = 2.3
GAMMA = 5.0 / 3.0
ROOT3 = 3.0**0.5
TINY = 1e-12
DIRECTIONS = [
    (dx, dy, dz) for dx in (-1, 0, 1) for dy in (-1, 0, 1) for dz in (-1, 0, 1) if (dx, dy, dz) != (0, 0, 0)
]
STEPS = [(a, b, c) for a in range(3) for b in range(3) for c in range(3)]


def source_part(step):
    return slice(2, 3) if step == 1 else slice(1, 2) if step == -1 else slice(1, 3)


def landing_part(step):
    return slice(0, 1) if step == 1 else slice(3, 4) if step == -1 else slice(1, 3)


def neighbour(direction):
    found = {}
    for axis, step in zip(AXES, direction):
        count = lax.axis_size(axis)
        found[axis] = lax.rem(lax.axis_index(axis) + count + step, count)
    return tuple(found[axis] for axis in AXES)


def inbox_part(step):
    return slice(0, 1) if step == 1 else slice(1, 2) if step == -1 else slice(0, 2)


def exchange(buffer, inbox, send_sem, recv_sem):
    copies = []
    for place, direction in enumerate(DIRECTIONS):
        if inbox is None:
            source = buffer.at[tuple(source_part(step) for step in direction)]
            target = buffer.at[tuple(landing_part(step) for step in direction)]
        else:
            source = buffer.at[tuple(landing_part(-step) for step in direction)]
            target = inbox.at[(place,) + tuple(inbox_part(step) for step in direction)]
        copies.append(
            pltpu.make_async_remote_copy(
                src_ref=source,
                dst_ref=target,
                send_sem=send_sem.at[place],
                recv_sem=recv_sem.at[place],
                device_id=neighbour(direction),
                device_id_type=MESH,
            )
        )
    return copies


def rounded(value):
    return value.astype(jnp.bfloat16).astype(jnp.float32)


def thirds(value):
    high = rounded(value)
    rest = value - high
    middle = rounded(rest)
    return high, middle, rest - middle


def cube_root(value):
    guess = jnp.exp(jnp.log(value) * (1.0 / 3.0))
    return (2.0 * guess + value / (guess * guess)) * (1.0 / 3.0)


def fold(tile):
    parts = [tile[8 * i : 8 * i + 8] for i in range(tile.shape[0] // 8)]
    while len(parts) > 1:
        parts = [parts[i] + parts[i + 1] for i in range(0, len(parts) - 1, 2)] + (
            [parts[-1]] if len(parts) % 2 else []
        )
    return parts[0]


def placed(tile, cell_x, cell_y, cell_z):
    row = lax.broadcasted_iota(jnp.int32, (8, 128), 0)
    shift = jnp.where(
        row == 0,
        jnp.float32(cell_x) - 2.0,
        jnp.where(row == 1, jnp.float32(cell_y) - 2.0, jnp.where(row == 2, jnp.float32(cell_z) - 2.0, 0.0)),
    )
    return row, tile + shift


def kernel(
    off_ref,
    mass_ref,
    smooth_ref,
    vel_ref,
    energy_ref,
    active_ref,
    dens_ref,
    acc_ref,
    heat_ref,
    field,
    outbox,
    inbox,
    feat,
    tfeat,
    state,
    mass_b,
    col_a,
    col_b,
    dist,
    square,
    total_ref,
    own_ref,
    react,
    send_sem,
    recv_sem,
    send_late,
    recv_late,
):
    f32 = jnp.float32
    barrier = pltpu.get_barrier_semaphore()
    for direction in DIRECTIONS:
        pl.semaphore_signal(barrier, inc=1, device_id=neighbour(direction), device_id_type=MESH)
    for x in range(2):
        for y in range(2):
            for z in range(2):
                for c in range(3):
                    field[1 + x, 1 + y, 1 + z, c : c + 1] = off_ref[c, x, y, z : z + 1]
                    field[1 + x, 1 + y, 1 + z, 4 + c : 5 + c] = vel_ref[c, x, y, z : z + 1]
                field[1 + x, 1 + y, 1 + z, 3:4] = mass_ref[x, y, z : z + 1]
                field[1 + x, 1 + y, 1 + z, 7:8] = energy_ref[x, y, z : z + 1]
    pl.semaphore_wait(barrier, len(DIRECTIONS))
    first = exchange(field, None, send_sem, recv_sem)
    for copy in first:
        copy.start()

    lane_row = lax.broadcasted_iota(jnp.int32, (48, 128), 0)
    pick = jnp.where((lane_row == 5) | (lane_row == 29) | (lane_row == 45), 1.0, 0.0).astype(jnp.bfloat16)

    def parts_of(target):
        return target // 4, (target // 2) % 2, target % 2

    def prepare(cell_x, cell_y, cell_z):
        cell = cell_x * 16 + cell_y * 4 + cell_z
        tile = field[cell_x, cell_y, cell_z]
        row, where_at = placed(tile, cell_x, cell_y, cell_z)
        mass = tile[3:4]
        norm = jnp.sum(jnp.where(row < 3, where_at * where_at, 0.0), axis=0, keepdims=True)
        moving = jnp.sum(jnp.where(row < 3, where_at * pltpu.roll(tile, 4, 0), 0.0), axis=0, keepdims=True)
        given = jnp.where(
            row < 3,
            where_at,
            jnp.where(row == 3, norm, jnp.where(row == 4, 1.0, jnp.where(row == 5, mass, 0.0))),
        )
        high, middle, low = thirds(given)
        stack = jnp.concatenate([high, high, high, middle, middle, low], axis=0)
        turned = jnp.transpose(stack).astype(jnp.bfloat16)
        feat[cell] = turned
        mass_b[cell] = jnp.dot(turned, pick, preferred_element_type=f32)
        column = jnp.where(row == 3, 1.0, jnp.where(row == 7, moving, where_at)) * mass
        high, middle, low = thirds(column)
        zero = jnp.zeros_like(low)
        upper = jnp.concatenate([high, middle, low, zero], axis=0).astype(jnp.bfloat16)
        lower = jnp.concatenate([high, middle, zero, zero], axis=0).astype(jnp.bfloat16)
        col_a[cell] = jnp.concatenate([upper, lower], axis=1)

    def prepare_own(target, carry):
        tx, ty, tz = parts_of(target)
        prepare(1 + tx, 1 + ty, 1 + tz)
        tile = field[1 + tx, 1 + ty, 1 + tz]
        row, where_at = placed(tile, 1 + tx, 1 + ty, 1 + tz)
        norm = jnp.sum(jnp.where(row < 3, where_at * where_at, 0.0), axis=0, keepdims=True)
        given = jnp.where(row < 3, -2.0 * where_at, jnp.where(row == 3, 1.0, jnp.where(row == 4, norm, 0.0)))
        high, middle, low = thirds(given)
        single = jnp.concatenate([high, middle, low, high, middle, high], axis=0)
        high, middle, low = thirds(3.0 * given)
        triple = jnp.concatenate([high, middle, low, high, middle, high], axis=0)
        tfeat[target] = jnp.concatenate([single, triple], axis=1).astype(jnp.bfloat16)
        return carry

    lax.fori_loop(0, 8, prepare_own, 0, unroll=2)

    def weigh(radius, three_square, length, half, half_cube):
        gap = jnp.maximum(length - radius, 0.0)
        return jnp.where(radius < half, half_cube - three_square * gap, gap * gap * gap)

    def remote_steps(target):
        tx, ty, tz = parts_of(target)
        steps = [(2 * tx, b, c) for b in range(3) for c in range(3)]
        steps += [(1 - tx + a, 2 * ty, c) for a in range(2) for c in range(3)]
        steps += [(1 - tx + a, 1 - ty + b, 2 * tz) for a in range(2) for b in range(2)]
        return steps

    def own_steps(target):
        tx, ty, tz = parts_of(target)
        return [(1 - tx + a, 1 - ty + b, 1 - tz + c) for a in range(2) for b in range(2) for c in range(2)]

    def cell_of(target, step):
        tx, ty, tz = parts_of(target)
        return (tx + step[0]) * 16 + (ty + step[1]) * 4 + (tz + step[2])

    def place_of(step):
        return step[0] * 9 + step[1] * 3 + step[2]

    def first_sum(target, steps):
        tx, ty, tz = parts_of(target)
        length = smooth_ref[tx, ty, pl.ds(tz, 1)]
        half = 0.5 * length
        half_cube = half * length * length
        target_feat = tfeat[target]
        total = jnp.zeros((8, 128), f32)
        for step in steps:
            cell, place = cell_of(target, step), place_of(step)
            both = jnp.dot(feat[cell], target_feat, preferred_element_type=f32)
            flat = jnp.maximum(both[:, :128], TINY)
            three_square = both[:, 128:]
            radius = flat * lax.rsqrt(flat)
            dist[target, place] = radius
            square[target, place] = three_square
            total = total + fold(mass_b[cell] * weigh(radius, three_square, length, half, half_cube))
        return length, total

    def first_own(target, carry):
        total_ref[target] = first_sum(target, own_steps(target))[1]
        return carry

    lax.fori_loop(0, 8, first_own, 0)

    for copy in first:
        copy.wait()

    for part, (low_x, high_x, low_y, high_y, low_z, high_z, step_x, step_y, step_z) in enumerate(
        [(0, 4, 0, 4, 0, 4, 3, 1, 1), (1, 3, 0, 4, 0, 4, 1, 3, 1), (1, 3, 1, 3, 0, 4, 1, 1, 3)]
    ):
        cells = [
            (x, y, z)
            for x in range(low_x, high_x, step_x)
            for y in range(low_y, high_y, step_y)
            for z in range(low_z, high_z, step_z)
        ]
        count_y, count_z = len(range(low_y, high_y, step_y)), len(range(low_z, high_z, step_z))

        def prepare_remote(index, carry):
            prepare(
                low_x + step_x * (index // (count_y * count_z)),
                low_y + step_y * (index // count_z % count_y),
                low_z + step_z * (index % count_z),
            )
            return carry

        lax.fori_loop(0, len(cells), prepare_remote, 0, unroll=4)

    def density_of(total, length):
        cube = length * length * length
        return (2.0 * KERNEL_NORM) * jnp.sum(total, axis=0, keepdims=True) / (cube * cube)

    def target_fields(target):
        tx, ty, tz = parts_of(target)
        tile = field[1 + tx, 1 + ty, 1 + tz]
        row, where_at = placed(tile, 1 + tx, 1 + ty, 1 + tz)
        return tile, row, where_at

    def first_rest(target, carry):
        length, total = first_sum(target, remote_steps(target))
        tile, row, where_at = target_fields(target)
        density = density_of(total_ref[target] + total, length)
        state[target, 0:1] = ETA * cube_root(tile[3:4] / density)
        return carry

    lax.fori_loop(0, 8, first_rest, 0)

    def second_pass(target, carry):
        tx, ty, tz = parts_of(target)
        length = state[target, 0:1]
        half = 0.5 * length
        half_cube = half * length * length

        def rows(index, total):
            for c in range(3):
                cell = (tx + index // 3) * 16 + (ty + index % 3) * 4 + tz + c
                place = index * 3 + c
                total = total + fold(
                    mass_b[cell] * weigh(dist[target, place], square[target, place], length, half, half_cube)
                )
            return total

        total = lax.fori_loop(0, 9, rows, jnp.zeros((8, 128), f32))
        tile, row, where_at = target_fields(target)
        mass, energy = tile[3:4], tile[7:8]
        density = density_of(total, length)
        length = ETA * cube_root(mass / density)
        dens_ref[tx, ty, pl.ds(tz, 1)] = density
        cube = length * length * length
        ratio = (GAMMA - 1.0) * energy / density / (cube * cube)
        state[target, 0:1] = length
        state[target, 1:2] = ratio
        column = jnp.where(row == 3, 1.0, jnp.where(row < 3, where_at, 0.0)) * (mass * ratio)
        high, middle, low = thirds(column)
        pair = jnp.where(row < 4, high, pltpu.roll(middle, 4, 0))
        upper = jnp.concatenate([pair, low], axis=0).astype(jnp.bfloat16)
        lower = jnp.concatenate([pair, jnp.zeros_like(low)], axis=0).astype(jnp.bfloat16)
        col_b[target] = jnp.concatenate([upper, lower], axis=1)
        return carry

    lax.fori_loop(0, 8, second_pass, 0)

    def clear(index, carry):
        react[index] = jnp.zeros((16, 128), f32)
        return carry

    lax.fori_loop(0, 64, clear, 0, unroll=8)

    def force(target, steps):
        length = state[target, 0:1]
        half = 0.5 * length
        steep = (2.0 / ROOT3) * length
        beta = col_b[target]
        own = jnp.zeros((32, 128), f32)
        for step in steps:
            cell, place = cell_of(target, step), place_of(step)
            radius = dist[target, place]
            inverse = lax.rsqrt(square[target, place])
            gap = jnp.maximum(length - radius, 0.0)
            slope = jnp.where(radius < half, steep - ROOT3 * radius, gap * gap * inverse)
            high = slope.astype(jnp.bfloat16)
            low = (slope - high.astype(f32)).astype(jnp.bfloat16)
            own = own + jnp.dot(col_a[cell], jnp.concatenate([high, low], axis=0), preferred_element_type=f32)
            react[cell] += lax.dot_general(
                beta,
                jnp.concatenate([high, low], axis=1),
                (((1,), (1,)), ((), ())),
                preferred_element_type=f32,
            )
        return own

    def settled(cell, tile, cell_x, cell_y, cell_z):
        row, where_at = placed(tile, cell_x, cell_y, cell_z)
        parts = react[cell]
        parts = parts[0:8] + (pltpu.roll(parts[0:8], 4, 0) + parts[8:16])
        return where_at * parts[3:4] - parts

    def force_remote(target, carry):
        own_ref[target] = force(target, remote_steps(target))
        return carry

    lax.fori_loop(0, 8, force_remote, 0)

    def post(cell, carry):
        cell_x, cell_y, cell_z = cell // 16, cell // 4 % 4, cell % 4
        outbox[cell_x, cell_y, cell_z] = settled(cell, field[cell_x, cell_y, cell_z], cell_x, cell_y, cell_z)[0:4]
        return carry

    lax.fori_loop(0, 64, post, 0, unroll=4)
    second = exchange(outbox, inbox, send_late, recv_late)
    for copy in second:
        copy.start()

    def force_own(target, carry):
        own_ref[target] += force(target, own_steps(target))
        return carry

    lax.fori_loop(0, 8, force_own, 0)

    for copy in second:
        copy.wait()

    for target in range(8):
        tx, ty, tz = target // 4, target // 2 % 2, target % 2
        tile = field[1 + tx, 1 + ty, 1 + tz]
        cell = (1 + tx) * 16 + (1 + ty) * 4 + 1 + tz
        row, where_at = placed(tile, 1 + tx, 1 + ty, 1 + tz)
        theirs = settled(cell, tile, 1 + tx, 1 + ty, 1 + tz)[0:4]
        for place, direction in enumerate(DIRECTIONS):
            spans = [inbox_part(step) for step in direction]
            if all(span.start <= at < span.stop for span, at in zip(spans, (tx, ty, tz))):
                theirs = theirs + inbox[place, tx, ty, tz]
        own = own_ref[target]
        own = own[0:8] + (own[8:16] + own[16:24])
        on = active_ref[tx, ty, tz : tz + 1].astype(f32)
        scale = (6.0 * ROOT3 * KERNEL_NORM) * on
        ratio = state[target, 1:2]
        bare = where_at * own[3:4] - own
        push = scale * (ratio * bare[0:3] + theirs[0:3])
        for c in range(3):
            acc_ref[c, tx, ty, tz : tz + 1] = push[c : c + 1]
        mixed = pltpu.roll(tile, 4, 0) * bare - where_at * pltpu.roll(own, 4, 0)
        heat = jnp.sum(jnp.where(row < 3, mixed, 0.0), axis=0, keepdims=True) + own[7:8]
        heat_ref[tx, ty, tz : tz + 1] = -scale * ratio * heat


def body(offsets, masses, smoothing, velocity, energy, active):
    f32, bf16 = jnp.float32, jnp.bfloat16
    vmem = pl.BlockSpec(memory_space=pltpu.VMEM)
    count = len(DIRECTIONS)
    return pl.pallas_call(
        kernel,
        out_shape=(
            jax.ShapeDtypeStruct(masses.shape, f32),
            jax.ShapeDtypeStruct(offsets.shape, f32),
            jax.ShapeDtypeStruct(masses.shape, f32),
        ),
        in_specs=[vmem] * 6,
        out_specs=(vmem, vmem, vmem),
        scratch_shapes=[
            pltpu.VMEM((4, 4, 4, 8, 128), f32),
            pltpu.VMEM((4, 4, 4, 4, 128), f32),
            pltpu.VMEM((count, 2, 2, 2, 4, 128), f32),
            pltpu.VMEM((64, 128, 48), bf16),
            pltpu.VMEM((8, 48, 256), bf16),
            pltpu.VMEM((8, 8, 128), f32),
            pltpu.VMEM((64, 128, 128), f32),
            pltpu.VMEM((64, 32, 256), bf16),
            pltpu.VMEM((8, 16, 256), bf16),
            pltpu.VMEM((8, 27, 128, 128), f32),
            pltpu.VMEM((8, 27, 128, 128), f32),
            pltpu.VMEM((8, 8, 128), f32),
            pltpu.VMEM((8, 32, 128), f32),
            pltpu.VMEM((64, 16, 128), f32),
            pltpu.SemaphoreType.DMA((count,)),
            pltpu.SemaphoreType.DMA((count,)),
            pltpu.SemaphoreType.DMA((count,)),
            pltpu.SemaphoreType.DMA((count,)),
        ],
        compiler_params=pltpu.CompilerParams(collective_id=0, has_side_effects=True, vmem_limit_bytes=60 * 1024 * 1024),
    )(offsets, masses, smoothing, velocity, energy, active)


def solution(mesh):
    in_specs = (
        P(None, "gx", "gy", "gz", None),
        P("gx", "gy", "gz", None),
        P("gx", "gy", "gz", None),
        P(None, "gx", "gy", "gz", None),
        P("gx", "gy", "gz", None),
        P("gx", "gy", "gz", None),
    )
    out_specs = (
        P("gx", "gy", "gz", None),
        P(None, "gx", "gy", "gz", None),
        P("gx", "gy", "gz", None),
    )
    return jax.shard_map(body, mesh=mesh, in_specs=in_specs, out_specs=out_specs, check_vma=False)
```

```python
import functools

import jax
import jax.numpy as jnp
from jax import lax
from jax.experimental import pallas as pl
from jax.experimental.pallas import tpu as pltpu
from jax.sharding import PartitionSpec as P

MESH = pl.DeviceIdType.MESH
AXES = ("gx", "gy", "gz")
KERNEL_NORM = 2.5464790894703255
ETA = 2.3
GAMMA = 5.0 / 3.0
ROOT3 = 3.0**0.5
TINY = 1e-7
DIRECTIONS = [
    (dx, dy, dz) for dx in (-1, 0, 1) for dy in (-1, 0, 1) for dz in (-1, 0, 1) if (dx, dy, dz) != (0, 0, 0)
]
STEPS = [(a, b, c) for a in range(3) for b in range(3) for c in range(3)]


def source_part(step):
    return slice(2, 3) if step == 1 else slice(1, 2) if step == -1 else slice(1, 3)


def landing_part(step):
    return slice(0, 1) if step == 1 else slice(3, 4) if step == -1 else slice(1, 3)


def rings():
    found = []
    for axis in AXES:
        count, me = lax.axis_size(axis), lax.axis_index(axis)
        found.append((me, lax.rem(me + 1, count), lax.rem(me + count - 1, count)))
    return found


def neighbour(ring, direction):
    return tuple(places[step] for places, step in zip(ring, direction))


def inbox_part(step):
    return slice(0, 1) if step == 1 else slice(1, 2) if step == -1 else slice(0, 2)


def exchange(ring, buffer, inbox, send_sem, recv_sem):
    copies = []
    for place, direction in enumerate(DIRECTIONS):
        if inbox is None:
            source = buffer.at[tuple(source_part(step) for step in direction)]
            target = buffer.at[tuple(landing_part(step) for step in direction)]
        else:
            source = buffer.at[tuple(landing_part(-step) for step in direction)]
            target = inbox.at[(place,) + tuple(inbox_part(step) for step in direction)]
        copies.append(
            pltpu.make_async_remote_copy(
                src_ref=source,
                dst_ref=target,
                send_sem=send_sem.at[place],
                recv_sem=recv_sem.at[place],
                device_id=neighbour(ring, direction),
                device_id_type=MESH,
            )
        )
    return copies


def rounded(value):
    return value.astype(jnp.bfloat16).astype(jnp.float32)


def thirds(value):
    high = rounded(value)
    rest = value - high
    middle = rounded(rest)
    return high, middle, rest - middle


def cube_root(value):
    guess = jnp.exp(jnp.log(value) * (1.0 / 3.0))
    return (2.0 * guess + value / (guess * guess)) * (1.0 / 3.0)


def fold(tile):
    parts = [tile[8 * i : 8 * i + 8] for i in range(tile.shape[0] // 8)]
    while len(parts) > 1:
        parts = [parts[i] + parts[i + 1] for i in range(0, len(parts) - 1, 2)] + (
            [parts[-1]] if len(parts) % 2 else []
        )
    return parts[0]


def placed(tile, cell_x, cell_y, cell_z):
    row = lax.broadcasted_iota(jnp.int32, (8, 128), 0)
    shift = jnp.where(
        row == 0,
        jnp.float32(cell_x) - 2.0,
        jnp.where(row == 1, jnp.float32(cell_y) - 2.0, jnp.where(row == 2, jnp.float32(cell_z) - 2.0, 0.0)),
    )
    return row, tile + shift


def kernel(
    off_ref,
    mass_ref,
    smooth_ref,
    vel_ref,
    energy_ref,
    out_ref,
    field,
    outbox,
    inbox,
    feat,
    tfeat,
    state,
    mass_b,
    col_a,
    col_b,
    dist,
    square,
    total_ref,
    own_ref,
    react,
    send_sem,
    recv_sem,
    send_late,
    recv_late,
):
    f32 = jnp.float32
    ring = rings()
    barrier = pltpu.get_barrier_semaphore()
    for direction in DIRECTIONS:
        pl.semaphore_signal(barrier, inc=1, device_id=neighbour(ring, direction), device_id_type=MESH)
    for x in range(2):
        for y in range(2):
            for z in range(2):
                for c in range(3):
                    field[1 + x, 1 + y, 1 + z, c : c + 1] = off_ref[c, x, y, z : z + 1]
                    field[1 + x, 1 + y, 1 + z, 4 + c : 5 + c] = vel_ref[c, x, y, z : z + 1]
                field[1 + x, 1 + y, 1 + z, 3:4] = mass_ref[x, y, z : z + 1]
                field[1 + x, 1 + y, 1 + z, 7:8] = energy_ref[x, y, z : z + 1]
    pl.semaphore_wait(barrier, len(DIRECTIONS))
    first = exchange(ring, field, None, send_sem, recv_sem)
    for copy in first:
        copy.start()

    lane_row = lax.broadcasted_iota(jnp.int32, (48, 128), 0)
    pick = jnp.where((lane_row == 5) | (lane_row == 29) | (lane_row == 45), 1.0, 0.0).astype(jnp.bfloat16)

    def parts_of(target):
        return target // 4, (target // 2) % 2, target % 2

    def prepare(cell_x, cell_y, cell_z):
        cell = cell_x * 16 + cell_y * 4 + cell_z
        tile = field[cell_x, cell_y, cell_z]
        row, where_at = placed(tile, cell_x, cell_y, cell_z)
        mass = tile[3:4]
        norm = jnp.sum(jnp.where(row < 3, where_at * where_at, 0.0), axis=0, keepdims=True)
        moving = jnp.sum(jnp.where(row < 3, where_at * pltpu.roll(tile, 4, 0), 0.0), axis=0, keepdims=True)
        given = jnp.where(
            row < 3,
            where_at,
            jnp.where(row == 3, norm, jnp.where(row == 4, 1.0, jnp.where(row == 5, mass, 0.0))),
        )
        high, middle, low = thirds(given)
        stack = jnp.concatenate([high, high, high, middle, middle, low], axis=0)
        turned = jnp.transpose(stack).astype(jnp.bfloat16)
        feat[cell] = turned
        mass_b[cell] = jnp.dot(turned, pick, preferred_element_type=f32)
        column = jnp.where(row == 3, 1.0, jnp.where(row == 7, moving, where_at)) * mass
        high, middle, low = thirds(column)
        zero = jnp.zeros_like(low)
        upper = jnp.concatenate([high, middle, low, zero], axis=0).astype(jnp.bfloat16)
        lower = jnp.concatenate([high, middle, zero, zero], axis=0).astype(jnp.bfloat16)
        col_a[cell] = jnp.concatenate([upper, lower], axis=1)

    def prepare_own(target, carry):
        tx, ty, tz = parts_of(target)
        prepare(1 + tx, 1 + ty, 1 + tz)
        tile = field[1 + tx, 1 + ty, 1 + tz]
        row, where_at = placed(tile, 1 + tx, 1 + ty, 1 + tz)
        norm = jnp.sum(jnp.where(row < 3, where_at * where_at, 0.0), axis=0, keepdims=True)
        given = jnp.where(row < 3, -2.0 * where_at, jnp.where(row == 3, 1.0, jnp.where(row == 4, norm, 0.0)))
        high, middle, low = thirds(given)
        single = jnp.concatenate([high, middle, low, high, middle, high], axis=0)
        high, middle, low = thirds(3.0 * given)
        triple = jnp.concatenate([high, middle, low, high, middle, high], axis=0)
        tfeat[target] = jnp.concatenate([single, triple], axis=1).astype(jnp.bfloat16)
        return carry

    lax.fori_loop(0, 8, prepare_own, 0, unroll=2)

    def weigh(radius, three_square, length, half, half_cube):
        gap = jnp.maximum(length - radius, 0.0)
        return jnp.where(radius < half, half_cube - three_square * gap, gap * gap * gap)

    def remote_steps(target):
        tx, ty, tz = parts_of(target)
        steps = [(2 * tx, b, c) for b in range(3) for c in range(3)]
        steps += [(1 - tx + a, 2 * ty, c) for a in range(2) for c in range(3)]
        steps += [(1 - tx + a, 1 - ty + b, 2 * tz) for a in range(2) for b in range(2)]
        return steps

    def own_steps(target):
        tx, ty, tz = parts_of(target)
        return [(1 - tx + a, 1 - ty + b, 1 - tz + c) for a in range(2) for b in range(2) for c in range(2)]

    def cell_of(target, step):
        tx, ty, tz = parts_of(target)
        return (tx + step[0]) * 16 + (ty + step[1]) * 4 + (tz + step[2])

    def place_of(step):
        return step[0] * 9 + step[1] * 3 + step[2]

    def first_sum(target, steps):
        tx, ty, tz = parts_of(target)
        length = smooth_ref[tx, ty, pl.ds(tz, 1)]
        half = 0.5 * length
        half_cube = half * length * length
        target_feat = tfeat[target]
        total = jnp.zeros((8, 128), f32)
        for step in steps:
            cell, place = cell_of(target, step), place_of(step)
            both = jnp.dot(feat[cell], target_feat, preferred_element_type=f32)
            for at in range(0, 128, 64):
                rows = slice(at, at + 64)
                flat = both[rows, :128]
                three_square = both[rows, 128:]
                radius = flat * lax.rsqrt(jnp.maximum(flat, TINY))
                dist[target, place, rows] = radius
                square[target, place, rows] = three_square
                total = total + fold(mass_b[cell, rows] * weigh(radius, three_square, length, half, half_cube))
        return length, total

    def first_own(target, carry):
        total_ref[target] = first_sum(target, own_steps(target))[1]
        return carry

    lax.fori_loop(0, 8, first_own, 0)

    for copy in first:
        copy.wait()

    def prepare_remote(side, carry):
        for y in range(4):
            for z in range(4):
                prepare(3 * side, y, z)
        for y in (0, 3):
            for z in range(4):
                prepare(1 + side, y, z)
        for y in (1, 2):
            for z in (0, 3):
                prepare(1 + side, y, z)
        return carry

    lax.fori_loop(0, 2, prepare_remote, 0)

    def density_of(total, length):
        cube = length * length * length
        return (2.0 * KERNEL_NORM) * jnp.sum(total, axis=0, keepdims=True) / (cube * cube)

    def target_fields(target):
        tx, ty, tz = parts_of(target)
        tile = field[1 + tx, 1 + ty, 1 + tz]
        row, where_at = placed(tile, 1 + tx, 1 + ty, 1 + tz)
        return tile, row, where_at

    def first_rest(target, carry):
        length, total = first_sum(target, remote_steps(target))
        tile, row, where_at = target_fields(target)
        density = density_of(total_ref[target] + total, length)
        state[target, 0:1] = ETA * cube_root(tile[3:4] / density)
        return carry

    lax.fori_loop(0, 8, first_rest, 0)

    def second_pass(target, carry):
        tx, ty, tz = parts_of(target)
        length = state[target, 0:1]
        half = 0.5 * length
        half_cube = half * length * length

        def rows(index, total):
            for at in range(9):
                cell = (tx + index) * 16 + (ty + at // 3) * 4 + tz + at % 3
                place = index * 9 + at
                for first_row in range(0, 128, 64):
                    at_rows = slice(first_row, first_row + 64)
                    near = weigh(
                        dist[target, place, at_rows], square[target, place, at_rows], length, half, half_cube
                    )
                    total = total + fold(mass_b[cell, at_rows] * near)
            return total

        total = lax.fori_loop(0, 3, rows, jnp.zeros((8, 128), f32))
        tile, row, where_at = target_fields(target)
        mass, energy = tile[3:4], tile[7:8]
        density = density_of(total, length)
        length = ETA * cube_root(mass / density)
        out_ref[0, tx, ty, pl.ds(tz, 1)] = density
        cube = length * length * length
        ratio = (GAMMA - 1.0) * energy / density / (cube * cube)
        state[target, 0:1] = length
        state[target, 1:2] = ratio
        column = jnp.where(row == 3, 1.0, jnp.where(row < 3, where_at, 0.0)) * (mass * ratio)
        high, middle, low = thirds(column)
        pair = jnp.where(row < 4, high, pltpu.roll(middle, 4, 0))
        upper = jnp.concatenate([pair, low], axis=0).astype(jnp.bfloat16)
        lower = jnp.concatenate([pair, jnp.zeros_like(low)], axis=0).astype(jnp.bfloat16)
        col_b[target] = jnp.concatenate([upper, lower], axis=1)
        return carry

    lax.fori_loop(0, 8, second_pass, 0)

    def clear(index, carry):
        react[pl.ds(16 * index, 16)] = jnp.zeros((16, 16, 128), f32)
        return carry

    lax.fori_loop(0, 4, clear, 0)

    def force(target, steps):
        length = state[target, 0:1]
        half = 0.5 * length
        steep = (2.0 / ROOT3) * length
        beta = col_b[target]
        own = jnp.zeros((32, 128), f32)
        for step in steps:
            cell, place = cell_of(target, step), place_of(step)
            highs, lows = [], []
            for at in range(0, 128, 64):
                radius = dist[target, place, at : at + 64]
                inverse = lax.rsqrt(square[target, place, at : at + 64])
                gap = jnp.maximum(length - radius, 0.0)
                slope = jnp.where(radius < half, steep - ROOT3 * radius, gap * gap * inverse)
                highs.append(slope.astype(jnp.bfloat16))
                lows.append((slope - highs[-1].astype(f32)).astype(jnp.bfloat16))
            high, low = jnp.concatenate(highs, axis=0), jnp.concatenate(lows, axis=0)
            own = own + jnp.dot(col_a[cell], jnp.concatenate([high, low], axis=0), preferred_element_type=f32)
            react[cell] += lax.dot_general(
                beta,
                jnp.concatenate([high, low], axis=1),
                (((1,), (1,)), ((), ())),
                preferred_element_type=f32,
            )
        return own

    def settled(cell, tile, cell_x, cell_y, cell_z):
        row, where_at = placed(tile, cell_x, cell_y, cell_z)
        parts = react[cell]
        parts = parts[0:8] + (pltpu.roll(parts[0:8], 4, 0) + parts[8:16])
        return where_at * parts[3:4] - parts

    def force_remote(target, carry):
        own_ref[target] = force(target, remote_steps(target))
        return carry

    lax.fori_loop(0, 8, force_remote, 0)

    def post(cell_x, carry):
        for y in range(4):
            for z in range(4):
                outbox[cell_x, y, z] = settled(cell_x * 16 + y * 4 + z, field[cell_x, y, z], cell_x, y, z)[0:4]
        return carry

    lax.fori_loop(0, 4, post, 0)
    second = exchange(ring, outbox, inbox, send_late, recv_late)
    for copy in second:
        copy.start()

    def force_own(target, carry):
        own_ref[target] += force(target, own_steps(target))
        return carry

    lax.fori_loop(0, 8, force_own, 0)

    for copy in second:
        copy.wait()

    for target in range(8):
        tx, ty, tz = target // 4, target // 2 % 2, target % 2
        tile = field[1 + tx, 1 + ty, 1 + tz]
        cell = (1 + tx) * 16 + (1 + ty) * 4 + 1 + tz
        row, where_at = placed(tile, 1 + tx, 1 + ty, 1 + tz)
        theirs = settled(cell, tile, 1 + tx, 1 + ty, 1 + tz)[0:4]
        for place, direction in enumerate(DIRECTIONS):
            spans = [inbox_part(step) for step in direction]
            if all(span.start <= at < span.stop for span, at in zip(spans, (tx, ty, tz))):
                theirs = theirs + inbox[place, tx, ty, tz]
        own = own_ref[target]
        own = own[0:8] + (own[8:16] + own[16:24])
        scale = 6.0 * ROOT3 * KERNEL_NORM
        ratio = state[target, 1:2]
        bare = where_at * own[3:4] - own
        push = scale * (ratio * bare[0:3] + theirs[0:3])
        for c in range(3):
            out_ref[1 + c, tx, ty, tz : tz + 1] = push[c : c + 1]
        mixed = pltpu.roll(tile, 4, 0) * bare - where_at * pltpu.roll(own, 4, 0)
        heat = jnp.sum(jnp.where(row < 3, mixed, 0.0), axis=0, keepdims=True) + own[7:8]
        out_ref[4, tx, ty, tz : tz + 1] = -scale * ratio * heat


def finish(result_ref, active_ref, dens_ref, acc_ref, heat_ref):
    on = active_ref[...].astype(jnp.float32)
    dens_ref[...] = result_ref[0]
    for c in range(3):
        acc_ref[c] = result_ref[1 + c] * on
    heat_ref[...] = result_ref[4] * on


def body(offsets, masses, smoothing, velocity, energy, active):
    f32, bf16 = jnp.float32, jnp.bfloat16
    vmem = pl.BlockSpec(memory_space=pltpu.VMEM)
    count = len(DIRECTIONS)
    result = pl.pallas_call(
        kernel,
        out_shape=jax.ShapeDtypeStruct((5,) + masses.shape, f32),
        in_specs=[vmem] * 5,
        out_specs=vmem,
        scratch_shapes=[
            pltpu.VMEM((4, 4, 4, 8, 128), f32),
            pltpu.VMEM((4, 4, 4, 4, 128), f32),
            pltpu.VMEM((count, 2, 2, 2, 4, 128), f32),
            pltpu.VMEM((64, 128, 48), bf16),
            pltpu.VMEM((8, 48, 256), bf16),
            pltpu.VMEM((8, 8, 128), f32),
            pltpu.VMEM((64, 128, 128), f32),
            pltpu.VMEM((64, 32, 256), bf16),
            pltpu.VMEM((8, 16, 256), bf16),
            pltpu.VMEM((8, 27, 128, 128), f32),
            pltpu.VMEM((8, 27, 128, 128), f32),
            pltpu.VMEM((8, 8, 128), f32),
            pltpu.VMEM((8, 32, 128), f32),
            pltpu.VMEM((64, 16, 128), f32),
            pltpu.SemaphoreType.DMA((count,)),
            pltpu.SemaphoreType.DMA((count,)),
            pltpu.SemaphoreType.DMA((count,)),
            pltpu.SemaphoreType.DMA((count,)),
        ],
        compiler_params=pltpu.CompilerParams(collective_id=0, has_side_effects=True, vmem_limit_bytes=60 * 1024 * 1024),
    )(offsets, masses, smoothing, velocity, energy)
    return pl.pallas_call(
        finish,
        out_shape=(
            jax.ShapeDtypeStruct(masses.shape, f32),
            jax.ShapeDtypeStruct(offsets.shape, f32),
            jax.ShapeDtypeStruct(masses.shape, f32),
        ),
        in_specs=[vmem] * 2,
        out_specs=(vmem, vmem, vmem),
    )(result, active)


def solution(mesh):
    in_specs = (
        P(None, "gx", "gy", "gz", None),
        P("gx", "gy", "gz", None),
        P("gx", "gy", "gz", None),
        P(None, "gx", "gy", "gz", None),
        P("gx", "gy", "gz", None),
        P("gx", "gy", "gz", None),
    )
    out_specs = (
        P("gx", "gy", "gz", None),
        P(None, "gx", "gy", "gz", None),
        P("gx", "gy", "gz", None),
    )
    return jax.shard_map(body, mesh=mesh, in_specs=in_specs, out_specs=out_specs, check_vma=False)
```

```python
import functools

import jax
import jax.numpy as jnp
from jax import lax
from jax.experimental import pallas as pl
from jax.experimental.pallas import tpu as pltpu
from jax.sharding import PartitionSpec as P

MESH = pl.DeviceIdType.MESH
AXES = ("gx", "gy", "gz")
KERNEL_NORM = 2.5464790894703255
ETA = 2.3
GAMMA = 5.0 / 3.0
ROOT3 = 3.0**0.5
TINY = 1e-7
DIRECTIONS = [
    (dx, dy, dz) for dx in (-1, 0, 1) for dy in (-1, 0, 1) for dz in (-1, 0, 1) if (dx, dy, dz) != (0, 0, 0)
]
STEPS = [(a, b, c) for a in range(3) for b in range(3) for c in range(3)]


def source_part(step):
    return slice(2, 3) if step == 1 else slice(1, 2) if step == -1 else slice(1, 3)


def landing_part(step):
    return slice(0, 1) if step == 1 else slice(3, 4) if step == -1 else slice(1, 3)


def rings():
    found = []
    for axis in AXES:
        count, me = lax.axis_size(axis), lax.axis_index(axis)
        found.append((me, lax.rem(me + 1, count), lax.rem(me + count - 1, count)))
    return found


def neighbour(ring, direction):
    return tuple(places[step] for places, step in zip(ring, direction))


def inbox_part(step):
    return slice(0, 1) if step == 1 else slice(1, 2) if step == -1 else slice(0, 2)


def exchange(ring, buffer, inbox, send_sem, recv_sem):
    copies = []
    for place, direction in enumerate(DIRECTIONS):
        if inbox is None:
            source = buffer.at[tuple(source_part(step) for step in direction)]
            target = buffer.at[tuple(landing_part(step) for step in direction)]
        else:
            source = buffer.at[tuple(landing_part(-step) for step in direction)]
            target = inbox.at[(place,) + tuple(inbox_part(step) for step in direction)]
        copies.append(
            pltpu.make_async_remote_copy(
                src_ref=source,
                dst_ref=target,
                send_sem=send_sem.at[place],
                recv_sem=recv_sem.at[place],
                device_id=neighbour(ring, direction),
                device_id_type=MESH,
            )
        )
    return copies


def rounded(value):
    return value.astype(jnp.bfloat16).astype(jnp.float32)


def thirds(value):
    high = rounded(value)
    rest = value - high
    middle = rounded(rest)
    return high, middle, rest - middle


def cube_root(value):
    guess = jnp.exp(jnp.log(value) * (1.0 / 3.0))
    return (2.0 * guess + value / (guess * guess)) * (1.0 / 3.0)


def fold(tile):
    parts = [tile[8 * i : 8 * i + 8] for i in range(tile.shape[0] // 8)]
    while len(parts) > 1:
        parts = [parts[i] + parts[i + 1] for i in range(0, len(parts) - 1, 2)] + (
            [parts[-1]] if len(parts) % 2 else []
        )
    return parts[0]


def placed(tile, cell_x, cell_y, cell_z):
    row = lax.broadcasted_iota(jnp.int32, (8, 128), 0)
    shift = jnp.where(
        row == 0,
        jnp.float32(cell_x) - 2.0,
        jnp.where(row == 1, jnp.float32(cell_y) - 2.0, jnp.where(row == 2, jnp.float32(cell_z) - 2.0, 0.0)),
    )
    return row, tile + shift


def kernel(
    off_ref,
    mass_ref,
    smooth_ref,
    vel_ref,
    energy_ref,
    out_ref,
    field,
    outbox,
    inbox,
    feat,
    tfeat,
    state,
    mass_b,
    col_a,
    col_b,
    dist,
    square,
    total_ref,
    own_ref,
    react,
    send_sem,
    recv_sem,
    send_late,
    recv_late,
):
    f32 = jnp.float32
    ring = rings()
    barrier = pltpu.get_barrier_semaphore()
    for direction in DIRECTIONS:
        pl.semaphore_signal(barrier, inc=1, device_id=neighbour(ring, direction), device_id_type=MESH)
    for x in range(2):
        for y in range(2):
            for z in range(2):
                for c in range(3):
                    field[1 + x, 1 + y, 1 + z, c : c + 1] = off_ref[c, x, y, z : z + 1]
                    field[1 + x, 1 + y, 1 + z, 4 + c : 5 + c] = vel_ref[c, x, y, z : z + 1]
                field[1 + x, 1 + y, 1 + z, 3:4] = mass_ref[x, y, z : z + 1]
                field[1 + x, 1 + y, 1 + z, 7:8] = energy_ref[x, y, z : z + 1]
    pl.semaphore_wait(barrier, len(DIRECTIONS))
    first = exchange(ring, field, None, send_sem, recv_sem)
    for copy in first:
        copy.start()

    lane_row = lax.broadcasted_iota(jnp.int32, (48, 128), 0)
    pick = jnp.where((lane_row == 5) | (lane_row == 29) | (lane_row == 45), 1.0, 0.0).astype(jnp.bfloat16)

    def parts_of(target):
        return target // 4, (target // 2) % 2, target % 2

    def prepare(cell_x, cell_y, cell_z):
        cell = cell_x * 16 + cell_y * 4 + cell_z
        tile = field[cell_x, cell_y, cell_z]
        row, where_at = placed(tile, cell_x, cell_y, cell_z)
        mass = tile[3:4]
        norm = jnp.sum(jnp.where(row < 3, where_at * where_at, 0.0), axis=0, keepdims=True)
        moving = jnp.sum(jnp.where(row < 3, where_at * pltpu.roll(tile, 4, 0), 0.0), axis=0, keepdims=True)
        given = jnp.where(
            row < 3,
            where_at,
            jnp.where(row == 3, norm, jnp.where(row == 4, 1.0, jnp.where(row == 5, mass, 0.0))),
        )
        high, middle, low = thirds(given)
        stack = jnp.concatenate([high, high, high, middle, middle, low], axis=0)
        turned = jnp.transpose(stack).astype(jnp.bfloat16)
        feat[cell] = turned
        mass_b[cell] = jnp.dot(turned, pick, preferred_element_type=f32)
        column = jnp.where(row == 3, 1.0, jnp.where(row == 7, moving, where_at)) * mass
        high, middle, low = thirds(column)
        zero = jnp.zeros_like(low)
        upper = jnp.concatenate([high, middle, low, zero], axis=0).astype(jnp.bfloat16)
        lower = jnp.concatenate([high, middle, zero, zero], axis=0).astype(jnp.bfloat16)
        col_a[cell] = jnp.concatenate([upper, lower], axis=1)

    def prepare_own(target, carry):
        tx, ty, tz = parts_of(target)
        prepare(1 + tx, 1 + ty, 1 + tz)
        tile = field[1 + tx, 1 + ty, 1 + tz]
        row, where_at = placed(tile, 1 + tx, 1 + ty, 1 + tz)
        norm = jnp.sum(jnp.where(row < 3, where_at * where_at, 0.0), axis=0, keepdims=True)
        given = jnp.where(row < 3, -2.0 * where_at, jnp.where(row == 3, 1.0, jnp.where(row == 4, norm, 0.0)))
        high, middle, low = thirds(given)
        single = jnp.concatenate([high, middle, low, high, middle, high], axis=0)
        high, middle, low = thirds(3.0 * given)
        triple = jnp.concatenate([high, middle, low, high, middle, high], axis=0)
        tfeat[target] = jnp.concatenate([single, triple], axis=1).astype(jnp.bfloat16)
        return carry

    lax.fori_loop(0, 8, prepare_own, 0, unroll=4)

    def weigh(radius, three_square, length, half, half_cube):
        gap = jnp.maximum(length - radius, 0.0)
        return jnp.where(radius < half, half_cube - three_square * gap, gap * gap * gap)

    def remote_steps(target):
        tx, ty, tz = parts_of(target)
        steps = [(2 * tx, b, c) for b in range(3) for c in range(3)]
        steps += [(1 - tx + a, 2 * ty, c) for a in range(2) for c in range(3)]
        steps += [(1 - tx + a, 1 - ty + b, 2 * tz) for a in range(2) for b in range(2)]
        return steps

    def own_steps(target):
        tx, ty, tz = parts_of(target)
        return [(1 - tx + a, 1 - ty + b, 1 - tz + c) for a in range(2) for b in range(2) for c in range(2)]

    def cell_of(target, step):
        tx, ty, tz = parts_of(target)
        return (tx + step[0]) * 16 + (ty + step[1]) * 4 + (tz + step[2])

    def place_of(step):
        return step[0] * 9 + step[1] * 3 + step[2]

    def first_sum(target, steps):
        tx, ty, tz = parts_of(target)
        length = smooth_ref[tx, ty, pl.ds(tz, 1)]
        half = 0.5 * length
        half_cube = half * length * length
        target_feat = tfeat[target]
        total = jnp.zeros((8, 128), f32)
        for step in steps:
            cell, place = cell_of(target, step), place_of(step)
            both = jnp.dot(feat[cell], target_feat, preferred_element_type=f32)
            flat, three_square = both[:, :128], both[:, 128:]
            radius = flat * lax.rsqrt(jnp.maximum(flat, TINY))
            dist[target, place] = radius
            square[target, place] = three_square
            total = total + fold(mass_b[cell] * weigh(radius, three_square, length, half, half_cube))
        return length, total

    def first_own(target, carry):
        total_ref[target] = first_sum(target, own_steps(target))[1]
        return carry

    lax.fori_loop(0, 8, first_own, 0, unroll=4)

    for copy in first:
        copy.wait()

    def prepare_remote(side, carry):
        for y in range(4):
            for z in range(4):
                prepare(3 * side, y, z)
        for y in (0, 3):
            for z in range(4):
                prepare(1 + side, y, z)
        for y in (1, 2):
            for z in (0, 3):
                prepare(1 + side, y, z)
        return carry

    lax.fori_loop(0, 2, prepare_remote, 0)

    def density_of(total, length):
        cube = length * length * length
        return (2.0 * KERNEL_NORM) * jnp.sum(total, axis=0, keepdims=True) / (cube * cube)

    def target_fields(target):
        tx, ty, tz = parts_of(target)
        tile = field[1 + tx, 1 + ty, 1 + tz]
        row, where_at = placed(tile, 1 + tx, 1 + ty, 1 + tz)
        return tile, row, where_at

    def first_rest(target, carry):
        length, total = first_sum(target, remote_steps(target))
        tile, row, where_at = target_fields(target)
        density = density_of(total_ref[target] + total, length)
        state[target, 0:1] = ETA * cube_root(tile[3:4] / density)
        return carry

    lax.fori_loop(0, 8, first_rest, 0, unroll=2)

    def second_pass(target, carry):
        tx, ty, tz = parts_of(target)
        length = state[target, 0:1]
        half = 0.5 * length
        half_cube = half * length * length

        def rows(index, total):
            for at in range(9):
                cell = (tx + index) * 16 + (ty + at // 3) * 4 + tz + at % 3
                place = index * 9 + at
                near = weigh(dist[target, place], square[target, place], length, half, half_cube)
                total = total + fold(mass_b[cell] * near)
            return total

        total = lax.fori_loop(0, 3, rows, jnp.zeros((8, 128), f32))
        tile, row, where_at = target_fields(target)
        mass, energy = tile[3:4], tile[7:8]
        density = density_of(total, length)
        length = ETA * cube_root(mass / density)
        out_ref[0, tx, ty, pl.ds(tz, 1)] = density
        cube = length * length * length
        ratio = (GAMMA - 1.0) * energy / density / (cube * cube)
        state[target, 0:1] = length
        state[target, 1:2] = ratio
        column = jnp.where(row == 3, 1.0, jnp.where(row < 3, where_at, 0.0)) * (mass * ratio)
        high, middle, low = thirds(column)
        pair = jnp.where(row < 4, high, pltpu.roll(middle, 4, 0))
        upper = jnp.concatenate([pair, low], axis=0).astype(jnp.bfloat16)
        lower = jnp.concatenate([pair, jnp.zeros_like(low)], axis=0).astype(jnp.bfloat16)
        col_b[target] = jnp.concatenate([upper, lower], axis=1)
        return carry

    lax.fori_loop(0, 8, second_pass, 0)

    def clear(index, carry):
        react[pl.ds(16 * index, 16)] = jnp.zeros((16, 16, 128), f32)
        return carry

    lax.fori_loop(0, 4, clear, 0)

    def force(target, steps):
        length = state[target, 0:1]
        half = 0.5 * length
        steep = (2.0 / ROOT3) * length
        beta = col_b[target]
        own = jnp.zeros((32, 128), f32)
        for step in steps:
            cell, place = cell_of(target, step), place_of(step)
            radius = dist[target, place]
            inverse = lax.rsqrt(square[target, place])
            gap = jnp.maximum(length - radius, 0.0)
            slope = jnp.where(radius < half, steep - ROOT3 * radius, gap * gap * inverse)
            high = slope.astype(jnp.bfloat16)
            low = (slope - high.astype(f32)).astype(jnp.bfloat16)
            own = own + jnp.dot(col_a[cell], jnp.concatenate([high, low], axis=0), preferred_element_type=f32)
            react[cell] += lax.dot_general(
                beta,
                jnp.concatenate([high, low], axis=1),
                (((1,), (1,)), ((), ())),
                preferred_element_type=f32,
            )
        return own

    def settled(cell, tile, cell_x, cell_y, cell_z):
        row, where_at = placed(tile, cell_x, cell_y, cell_z)
        parts = react[cell]
        parts = parts[0:8] + (pltpu.roll(parts[0:8], 4, 0) + parts[8:16])
        return where_at * parts[3:4] - parts

    def force_remote(target, carry):
        own_ref[target] = force(target, remote_steps(target))
        return carry

    lax.fori_loop(0, 8, force_remote, 0, unroll=2)

    def post(cell_x, carry):
        for y in range(4):
            for z in range(4):
                outbox[cell_x, y, z] = settled(cell_x * 16 + y * 4 + z, field[cell_x, y, z], cell_x, y, z)[0:4]
        return carry

    lax.fori_loop(0, 4, post, 0)
    second = exchange(ring, outbox, inbox, send_late, recv_late)
    for copy in second:
        copy.start()

    def force_own(target, carry):
        own_ref[target] += force(target, own_steps(target))
        return carry

    lax.fori_loop(0, 8, force_own, 0, unroll=4)

    for copy in second:
        copy.wait()

    for target in range(8):
        tx, ty, tz = target // 4, target // 2 % 2, target % 2
        tile = field[1 + tx, 1 + ty, 1 + tz]
        cell = (1 + tx) * 16 + (1 + ty) * 4 + 1 + tz
        row, where_at = placed(tile, 1 + tx, 1 + ty, 1 + tz)
        theirs = settled(cell, tile, 1 + tx, 1 + ty, 1 + tz)[0:4]
        for place, direction in enumerate(DIRECTIONS):
            spans = [inbox_part(step) for step in direction]
            if all(span.start <= at < span.stop for span, at in zip(spans, (tx, ty, tz))):
                theirs = theirs + inbox[place, tx, ty, tz]
        own = own_ref[target]
        own = own[0:8] + (own[8:16] + own[16:24])
        scale = 6.0 * ROOT3 * KERNEL_NORM
        ratio = state[target, 1:2]
        bare = where_at * own[3:4] - own
        push = scale * (ratio * bare[0:3] + theirs[0:3])
        for c in range(3):
            out_ref[1 + c, tx, ty, tz : tz + 1] = push[c : c + 1]
        mixed = pltpu.roll(tile, 4, 0) * bare - where_at * pltpu.roll(own, 4, 0)
        heat = jnp.sum(jnp.where(row < 3, mixed, 0.0), axis=0, keepdims=True) + own[7:8]
        out_ref[4, tx, ty, tz : tz + 1] = -scale * ratio * heat


def finish(result_ref, active_ref, dens_ref, acc_ref, heat_ref):
    on = active_ref[...].astype(jnp.float32)
    dens_ref[...] = result_ref[0]
    for c in range(3):
        acc_ref[c] = result_ref[1 + c] * on
    heat_ref[...] = result_ref[4] * on


def body(offsets, masses, smoothing, velocity, energy, active):
    f32, bf16 = jnp.float32, jnp.bfloat16
    vmem = pl.BlockSpec(memory_space=pltpu.VMEM)
    count = len(DIRECTIONS)
    result = pl.pallas_call(
        kernel,
        out_shape=jax.ShapeDtypeStruct((5,) + masses.shape, f32),
        in_specs=[vmem] * 5,
        out_specs=vmem,
        scratch_shapes=[
            pltpu.VMEM((4, 4, 4, 8, 128), f32),
            pltpu.VMEM((4, 4, 4, 4, 128), f32),
            pltpu.VMEM((count, 2, 2, 2, 4, 128), f32),
            pltpu.VMEM((64, 128, 48), bf16),
            pltpu.VMEM((8, 48, 256), bf16),
            pltpu.VMEM((8, 8, 128), f32),
            pltpu.VMEM((64, 128, 128), f32),
            pltpu.VMEM((64, 32, 256), bf16),
            pltpu.VMEM((8, 16, 256), bf16),
            pltpu.VMEM((8, 27, 128, 128), f32),
            pltpu.VMEM((8, 27, 128, 128), f32),
            pltpu.VMEM((8, 8, 128), f32),
            pltpu.VMEM((8, 32, 128), f32),
            pltpu.VMEM((64, 16, 128), f32),
            pltpu.SemaphoreType.DMA((count,)),
            pltpu.SemaphoreType.DMA((count,)),
            pltpu.SemaphoreType.DMA((count,)),
            pltpu.SemaphoreType.DMA((count,)),
        ],
        compiler_params=pltpu.CompilerParams(collective_id=0, has_side_effects=True, vmem_limit_bytes=60 * 1024 * 1024),
    )(offsets, masses, smoothing, velocity, energy)
    return pl.pallas_call(
        finish,
        out_shape=(
            jax.ShapeDtypeStruct(masses.shape, f32),
            jax.ShapeDtypeStruct(offsets.shape, f32),
            jax.ShapeDtypeStruct(masses.shape, f32),
        ),
        in_specs=[vmem] * 2,
        out_specs=(vmem, vmem, vmem),
    )(result, active)


def solution(mesh):
    in_specs = (
        P(None, "gx", "gy", "gz", None),
        P("gx", "gy", "gz", None),
        P("gx", "gy", "gz", None),
        P(None, "gx", "gy", "gz", None),
        P("gx", "gy", "gz", None),
        P("gx", "gy", "gz", None),
    )
    out_specs = (
        P("gx", "gy", "gz", None),
        P(None, "gx", "gy", "gz", None),
        P("gx", "gy", "gz", None),
    )
    return jax.shard_map(body, mesh=mesh, in_specs=in_specs, out_specs=out_specs, check_vma=False)
```
